32 devices in a mesh: grp: 2 (over y), seq: 4 (over z), sub: 2 (over x), rep: 2 (over core).
Axes of the slice: x: 2, y: 2, z: 4, core: 2. Of those that a mesh axis runs over, the one named last changes fastest.
Arguments:
- query_proj: bfloat16 [2048, 1536], P(('grp', 'seq'), ('sub', 'rep')), parts along dimension 0, may hold values from -5 to 5
- key_proj: bfloat16 [2048, 1536], P(('grp', 'seq'), ('sub', 'rep')), parts along dimension 0, may hold values from -5 to 5
- value_proj: bfloat16 [2048, 1536], P(('grp', 'seq'), ('sub', 'rep')), parts along dimension 0, may hold values from -8 to 8
- block_mask: int32 [24, 8, 8], P(('grp', 'sub', 'rep')), parts along dimension 0, may hold values from 0 to 1, as said below
- unit_plan: int32 [8, 4, 3], P(('grp', 'sub', 'rep')), parts along dimension 0, may hold values from 0 to 8, as said below
- out_weight: bfloat16 [1536, 3072], P(('sub', 'rep')), may hold values from -0.15625 to 0.15625
Outputs:
- attn_out: bfloat16 [2048, 3072], P(('grp', 'seq', 'sub', 'rep')), parts along dimension 0
- unit_logsum: float32 [8, 4, 1024], P(('grp', 'sub', 'rep'), 'seq'), parts along dimension 0
The draws below stay inside these ranges and needn't reach their ends.
There are 2 independent parts, one for each index of `grp`. The reference program is written for one: setup_inputs(seed, part) draws one part's arguments, and reference() takes and returns one part's arrays. A program takes and returns all parts, laid end to end along the dimension named above; an argument that names none is the same for every part. Nothing has to cross between parts.
Inputs may be any that keep to these rules, and one draw needn't show every extreme that they name: block_mask[h, b, b] = 1 for every head and block; every row holds 1 to 4 ones, and every head has a row with exactly 4. unit_plan[g, d] = (h, b, n): the device of index d along seq in head group g owns head h of the group's 3 heads, query blocks b to b + n - 1. For every head the units of the group cover its 8 query blocks exactly once; every head has at least one unit; n is 1 to 8, and some unit of every group has exactly 8.
All inputs are finite; a program needn't handle non-finite values.
Results may differ from the reference program's by a relative error of at most 0.0075.
Values may be sent and summed in bfloat16 or wider, within the bound.
A program may use at most 128 MiB of HBM per device.

```python
import math
import jax
import jax.numpy as jnp
from jax import lax

D = 3072
DH = 128
HEAD_DEV = 3
BLK = 128
HEADS = 12
TOKENS = 1024
NQB = 8
HGROUPS = 4
SLAB_MAX = 8
KMAX = 4
N_SEQ = 4


def query_key_pair(key):
    key_noise = jax.random.fold_in(key, 11)
    query_noise = jax.random.fold_in(key, 12)
    shape_full = (TOKENS, HEADS * DH)
    keys_drawn = jnp.clip(1.5 * jax.random.normal(key_noise, shape_full, jnp.float32), -5.0, 5.0)
    queries_drawn = jnp.clip(1.5 * jax.random.normal(query_noise, shape_full, jnp.float32), -5.0, 5.0)
    return (queries_drawn, keys_drawn)


def draw_query_proj(key, part):
    return query_key_pair(key)[0].astype(jnp.bfloat16)


def draw_key_proj(key, part):
    return query_key_pair(key)[1].astype(jnp.bfloat16)


def draw_block_mask(key, part):
    percent = jax.random.randint(jax.random.fold_in(key, 1), (HEADS, 1), 5, 31)
    upper_bound = percent * NQB * 4 // 300 + 1
    counts = 1 + jax.random.randint(jax.random.fold_in(key, 2), (HEADS, NQB), 0, upper_bound)
    forced = jax.random.randint(jax.random.fold_in(key, 3), (HEADS, 1), 0, NQB)
    counts = jnp.where(jnp.arange(NQB, dtype=jnp.int32)[None, :] == forced, KMAX, counts)
    ranking = jax.random.randint(jax.random.fold_in(key, 4), (HEADS, NQB, NQB), 0, 2 ** 30)
    diagonal = jnp.eye(NQB, dtype=bool)[None, :, :]
    ranking = jnp.where(diagonal, -1, ranking)
    positions = jnp.argsort(jnp.argsort(ranking, axis=-1, stable=True), axis=-1, stable=True)
    return (positions < counts[:, :, None]).astype(jnp.int32)


def one_plan(key):
    device_total = N_SEQ
    head_total = HEAD_DEV
    block_total = NQB
    most_blocks = SLAB_MAX
    base_count = device_total // head_total
    spare_count = device_total % head_total
    head_order = jax.random.permutation(jax.random.fold_in(key, 1), head_total)
    devices = base_count + (head_order < spare_count).astype(jnp.int32)
    source_head = jax.random.randint(jax.random.fold_in(key, 2), (), 0, head_total)
    target_head = (source_head + 1 + jax.random.randint(jax.random.fold_in(key, 3), (), 0, max(head_total - 1, 1))) % head_total
    moved = jax.random.randint(jax.random.fold_in(key, 4), (), 0, base_count // 3 + 1)
    head_ids = jnp.arange(head_total, dtype=jnp.int32)
    devices = devices - jnp.where(head_ids == source_head, moved, 0) + jnp.where(head_ids == target_head, moved, 0)
    largest = jnp.minimum(most_blocks, block_total - devices + 1)
    others = jnp.maximum(devices - 1, 1)
    rest_blocks = block_total - largest
    even_share = rest_blocks // others
    extra_share = rest_blocks % others
    big_place = jax.random.randint(jax.random.fold_in(key, 5), (head_total,), 0, devices)
    ends = jnp.cumsum(devices)
    begins = ends - devices
    slot_ids = jnp.arange(device_total, dtype=jnp.int32)
    head_of = jnp.sum((slot_ids[:, None] >= ends[None, :]).astype(jnp.int32), axis=1)
    rank_in = slot_ids - begins[head_of]
    big_rank = big_place[head_of]
    after_big = rank_in - (rank_in > big_rank).astype(jnp.int32)
    slab_length = jnp.where(rank_in == big_rank, largest[head_of], even_share[head_of] + (after_big < extra_share[head_of]).astype(jnp.int32))
    slab_first = jnp.cumsum(slab_length) - slab_length - head_of * block_total
    plan_rows = jnp.stack([head_of, slab_first, slab_length], axis=1).astype(jnp.int32)
    device_order = jax.random.permutation(jax.random.fold_in(key, 6), device_total)
    return plan_rows[device_order]


def draw_unit_plan(key, part):
    return jax.vmap(lambda group_id: one_plan(jax.random.fold_in(key, group_id)))(jnp.arange(HGROUPS, dtype=jnp.int32))


def block_levels(stream_key, extent, cuts, smallest, high):
    def one(position, blocks):
        heights = jax.random.uniform(jax.random.fold_in(jax.random.fold_in(stream_key, 6), position), (blocks,), jnp.float32, smallest / len(cuts), high / len(cuts))
        return jnp.repeat(jnp.exp(heights), extent[position] // blocks).reshape((-1,) + (1,) * (len(extent) - position - 1))

    factor_of = one(*cuts[0])
    for cut in cuts[1:]:
        factor_of = factor_of * one(*cut)
    return factor_of


def bell_draw(stream_key, shape, scale, bound, shards=(), held_as=jnp.bfloat16):
    drawn = scale * jax.random.normal(stream_key, shape, jnp.float32)
    if shards:
        drawn = drawn * block_levels(stream_key, shape, shards, -0.22, 0.18)
    return jnp.clip(drawn, -bound, bound).astype(held_as)


def setup_inputs(seed: int = 0, part: int = 0) -> dict:
    streams_of = jax.random.split(jax.random.key(seed), 7)
    part_splits = jax.random.split(jax.random.fold_in(streams_of[6], part), 7)
    return {
        "query_proj": draw_query_proj(jax.random.fold_in(jax.random.fold_in(streams_of[6], part), 71), part),
        "key_proj": draw_key_proj(jax.random.fold_in(jax.random.fold_in(streams_of[6], part), 71), part),
        "value_proj": bell_draw(part_splits[2], (TOKENS, HEADS * DH), 2.0, 8.0, ((0, 4), (1, 4))),
        "block_mask": draw_block_mask(jax.random.fold_in(jax.random.fold_in(streams_of[6], part), 71), part),
        "unit_plan": draw_unit_plan(jax.random.fold_in(jax.random.fold_in(streams_of[6], part), 71), part),
        "out_weight": bell_draw(streams_of[5], (HEADS * DH, D), (HEADS * DH) ** -0.5, 0.15625, ((0, 4),)),
    }


def head_attention(head_inputs):
    head_queries, head_keys, head_values, head_mask = head_inputs
    score_scale = 1.0 / math.sqrt(DH)
    query_blocks = head_queries.reshape(NQB, BLK, DH)

    def one_block(block_inputs):
        block_queries, mask_row = block_inputs
        key_live = jnp.repeat(mask_row > 0, BLK)[None, :]
        scores = jnp.dot(block_queries, head_keys.T, preferred_element_type=jnp.float32) * score_scale
        masked = jnp.where(key_live, scores, -jnp.inf)
        row_peak = lax.optimization_barrier(jnp.max(masked, axis=1, keepdims=True))
        weights = jnp.where(key_live, jnp.exp(masked - row_peak), 0.0)
        row_total = lax.optimization_barrier(jnp.sum(weights, axis=1, keepdims=True))
        mixed_rows = jnp.dot(weights.astype(jnp.bfloat16), head_values, preferred_element_type=jnp.float32) / row_total
        return (mixed_rows.astype(jnp.bfloat16), (row_peak + jnp.log(row_total))[:, 0])
    mixed_blocks, block_norms = lax.map(one_block, (query_blocks, head_mask))
    return (mixed_blocks.reshape(TOKENS, DH), block_norms.reshape(TOKENS))

def reference(query_proj, key_proj, value_proj, block_mask, unit_plan, out_weight):

    def split_heads(array):
        return array.reshape(TOKENS, HEADS, DH).transpose(1, 0, 2)
    mixed, lognorm = lax.map(head_attention, (split_heads(query_proj), split_heads(key_proj), split_heads(value_proj), block_mask))
    attn_rows = mixed.transpose(1, 0, 2).reshape(TOKENS, HEADS * DH)
    attn_out = jnp.dot(attn_rows, out_weight, preferred_element_type=jnp.float32).astype(jnp.bfloat16)
    padded_norm = jnp.concatenate([lognorm, jnp.zeros((HEADS, SLAB_MAX * BLK), lognorm.dtype)], axis=1)
    group_heads = jnp.arange(HGROUPS, dtype=jnp.int32)[:, None] * HEAD_DEV + unit_plan[:, :, 0]
    slab_rows = jnp.arange(SLAB_MAX * BLK, dtype=jnp.int32)[None, None, :]
    row_index = unit_plan[:, :, 1:2] * BLK + slab_rows
    row_valid = slab_rows < unit_plan[:, :, 2:3] * BLK
    unit_logsum = jnp.where(row_valid, padded_norm[group_heads[:, :, None], row_index], 0.0)
    return (attn_out, unit_logsum)
```

```python
import math

import jax
import jax.numpy as jnp
from jax import lax
from jax.sharding import PartitionSpec as P

DH = 128
BLK = 128


def by_owner(local_rows, owners):
    result = jnp.zeros(
        (owners.shape[0],) + local_rows.shape[:1] + local_rows.shape[2:], local_rows.dtype
    )
    for which_head in range(local_rows.shape[1]):
        matches = (owners == which_head).reshape((-1,) + (1,) * (local_rows.ndim - 1))
        result = jnp.where(matches, local_rows[:, which_head][None], result)
    return result


def key_lists_of(mask_rows, key_most):
    key_order = jnp.argsort(1 - mask_rows, axis=1, stable=True)[:, :key_most]
    live_slots = jnp.take_along_axis(mask_rows, key_order, axis=1) > 0
    return (key_order, live_slots)


def attend(
    query_units, blocks, key_slot, value_slot, key_lists, unit_heads, live_slots, unit_count
):
    unit_group = 4
    key_most = key_lists.shape[1]
    score_scale = 1.0 / math.sqrt(DH)
    out_init = jnp.zeros(query_units.shape, jnp.bfloat16)
    norm_init = jnp.zeros(query_units.shape[:2], jnp.float32)

    def one_turn(turn_index, loop_carry):
        outputs, lognorm = loop_carry
        first_unit = turn_index * unit_group
        group_queries = lax.dynamic_slice_in_dim(query_units, first_unit, unit_group, 0)
        group_rows = lax.dynamic_slice_in_dim(key_lists, first_unit, unit_group, 0)
        group_heads = lax.dynamic_slice_in_dim(unit_heads, first_unit, unit_group, 0)
        group_live = lax.dynamic_slice_in_dim(live_slots, first_unit, unit_group, 0)
        picked_keys = blocks[group_rows, :, group_heads[:, None], key_slot].reshape(
            unit_group, key_most * BLK, DH
        )
        picked_values = blocks[group_rows, :, group_heads[:, None], value_slot].reshape(
            unit_group, key_most * BLK, DH
        )
        scores = (
            jnp.einsum(
                "utc,ukc->utk", group_queries, picked_keys, preferred_element_type=jnp.float32
            )
            * score_scale
        )
        columns = jnp.repeat(group_live, BLK, axis=1)[:, None, :]
        masked = jnp.where(columns, scores, -jnp.inf)
        row_peak = jnp.max(masked, axis=2, keepdims=True)
        weights = jnp.where(columns, jnp.exp(masked - row_peak), 0.0)
        row_total = jnp.sum(weights, axis=2, keepdims=True)
        mixed_rows = (
            jnp.einsum(
                "utk,ukc->utc",
                weights.astype(jnp.bfloat16),
                picked_values,
                preferred_element_type=jnp.float32,
            )
            / row_total
        )
        outputs = lax.dynamic_update_slice_in_dim(
            outputs, mixed_rows.astype(jnp.bfloat16), first_unit, 0
        )
        lognorm = lax.dynamic_update_slice_in_dim(
            lognorm, (row_peak + jnp.log(row_total))[:, :, 0], first_unit, 0
        )
        return (outputs, lognorm)

    turn_total = (unit_count + unit_group - 1) // unit_group
    return lax.fori_loop(0, turn_total, one_turn, (out_init, norm_init))


def local(query_proj, key_proj, value_proj, block_mask, unit_plan, out_weight):
    tok_count = query_proj.shape[0]
    head_count = block_mask.shape[0]
    block_count = block_mask.shape[2]
    seq_count = lax.axis_size("seq")
    seq_index = lax.axis_index("seq")
    local_blocks = tok_count // BLK
    slab_most = min(2 * head_count * local_blocks, block_count)
    key_most = 2 * block_count // 5 + 1
    seq_tokens = seq_count * tok_count
    slab_units = -(-slab_most // 4) * 4
    owners = unit_plan[0, :, 0]
    firsts = unit_plan[0, :, 1]
    lengths = unit_plan[0, :, 2]
    own_head = owners[seq_index]
    own_first = firsts[seq_index]
    own_length = lengths[seq_index]
    query_local = query_proj.reshape(tok_count, head_count, DH)
    key_local = key_proj.reshape(tok_count, head_count, DH)
    value_local = value_proj.reshape(tok_count, head_count, DH)
    positions = seq_index * tok_count + jnp.arange(tok_count, dtype=jnp.int32)
    inside = (positions[None, :] >= firsts[:, None] * BLK) & (
        positions[None, :] < (firsts + lengths)[:, None] * BLK
    )
    filler = jnp.broadcast_to(
        (jnp.arange(block_count) == 0).astype(jnp.int32)[None, :], (slab_units, block_count)
    )
    sent_rows = by_owner(jnp.stack([key_local, value_local], axis=2), owners)
    arrived = lax.all_to_all(sent_rows, "seq", split_axis=0, concat_axis=0, tiled=True)
    blocks = arrived.reshape(block_count, BLK, 1, 2, DH)
    sent_queries = jnp.where(
        inside[:, :, None], by_owner(query_local, owners), jnp.zeros((), jnp.bfloat16)
    )
    head_queries = lax.all_to_all(
        sent_queries, "seq", split_axis=0, concat_axis=0, tiled=True
    ).reshape(seq_tokens, DH)
    key_slot = 0
    value_slot = 1
    head_queries = jnp.concatenate(
        [head_queries, jnp.zeros((slab_units * BLK, DH), jnp.bfloat16)], axis=0
    )
    query_units = lax.dynamic_slice_in_dim(
        head_queries, own_first * BLK, slab_units * BLK, 0
    ).reshape(slab_units, BLK, DH)
    head_mask = jnp.concatenate([block_mask[own_head], filler], axis=0)
    own_rows = lax.dynamic_slice_in_dim(head_mask, own_first, slab_units, 0)
    key_lists, live_slots = key_lists_of(own_rows, key_most)
    unit_heads = jnp.zeros((slab_units,), jnp.int32)
    outputs, lognorm = attend(
        query_units, blocks, key_slot, value_slot, key_lists, unit_heads, live_slots, own_length
    )
    unit_valid = jnp.arange(slab_units, dtype=jnp.int32) < own_length
    outputs = jnp.where(unit_valid[:, None, None], outputs, jnp.zeros((), jnp.bfloat16))
    unit_norm = jnp.where(unit_valid[:, None], lognorm, 0.0).reshape(slab_most * BLK)
    spread = jnp.zeros((seq_tokens + slab_units * BLK, DH), jnp.bfloat16)
    spread = lax.dynamic_update_slice_in_dim(
        spread, outputs.reshape(slab_units * BLK, DH), own_first * BLK, 0
    )
    returned = lax.all_to_all(
        spread[:seq_tokens].reshape(seq_count, tok_count, DH),
        "seq",
        split_axis=0,
        concat_axis=0,
        tiled=True,
    )
    head_picks = (owners[:, None] == jnp.arange(head_count, dtype=jnp.int32)[None, :]).astype(
        jnp.bfloat16
    )
    attn_local = (
        jnp.einsum("dh,dtc->thc", head_picks, returned, preferred_element_type=jnp.float32)
        .astype(jnp.bfloat16)
        .reshape(tok_count, head_count * DH)
    )
    summed = lax.psum_scatter(
        jnp.dot(attn_local, out_weight, preferred_element_type=jnp.float32).astype(jnp.bfloat16),
        ("sub", "rep"),
        scatter_dimension=0,
        tiled=True,
    )
    return (summed, unit_norm.reshape(1, 1, slab_most * BLK))


def solution(mesh):
    placed = (
        P(("grp", "seq"), ("sub", "rep")),
        P(("grp", "seq"), ("sub", "rep")),
        P(("grp", "seq"), ("sub", "rep")),
        P(("grp", "sub", "rep"), None, None),
        P(("grp", "sub", "rep"), None, None),
        P(("sub", "rep"), None),
    )
    return jax.shard_map(
        local,
        mesh=mesh,
        in_specs=placed,
        out_specs=(P(("grp", "seq", "sub", "rep"), None), P(("grp", "sub", "rep"), "seq", None)),
        check_vma=False,
    )
```

```python
import math

import jax
import jax.numpy as jnp
from jax import lax
from jax.sharding import PartitionSpec as P

DH = 128
BLK = 128


def local(query_proj, key_proj, value_proj, block_mask, unit_plan, out_weight):
    tok_count = query_proj.shape[0]
    head_count = block_mask.shape[0]
    block_count = block_mask.shape[2]
    seq_index = lax.axis_index("seq")
    local_blocks = tok_count // BLK
    slab_most = min(2 * head_count * local_blocks, block_count)
    score_scale = 1.0 / math.sqrt(DH)
    key_value = jnp.stack([key_proj, value_proj], axis=0)
    gathered = lax.all_gather(key_value, "seq", axis=1, tiled=True)
    all_tokens = gathered.shape[1]
    keys = gathered[0].reshape(all_tokens, head_count, DH)
    values = gathered[1].reshape(all_tokens, head_count, DH)
    queries = query_proj.reshape(tok_count, head_count, DH)
    scores = (
        jnp.einsum("thc,shc->hts", queries, keys, preferred_element_type=jnp.float32)
        * score_scale
    )
    own_rows = lax.dynamic_slice_in_dim(block_mask, seq_index * local_blocks, local_blocks, 1)
    live = jnp.repeat(jnp.repeat(own_rows > 0, BLK, axis=1), BLK, axis=2)
    masked = jnp.where(live, scores, -jnp.inf)
    row_peak = jnp.max(masked, axis=2, keepdims=True)
    weights = jnp.where(live, jnp.exp(masked - row_peak), 0.0)
    row_total = jnp.sum(weights, axis=2, keepdims=True)
    mixed = (
        jnp.einsum(
            "hts,shc->htc",
            weights.astype(jnp.bfloat16),
            values,
            preferred_element_type=jnp.float32,
        )
        / row_total
    )
    attn_local = mixed.astype(jnp.bfloat16).transpose(1, 0, 2).reshape(tok_count, head_count * DH)
    lognorm = (row_peak + jnp.log(row_total))[:, :, 0]
    all_norm = lax.all_gather(lognorm, "seq", axis=1, tiled=True)
    own_head = unit_plan[0, seq_index, 0]
    own_first = unit_plan[0, seq_index, 1]
    own_length = unit_plan[0, seq_index, 2]
    head_norm = jnp.concatenate(
        [all_norm[own_head], jnp.zeros((slab_most * BLK,), jnp.float32)], axis=0
    )
    unit_norm = lax.dynamic_slice_in_dim(head_norm, own_first * BLK, slab_most * BLK, 0)
    unit_norm = jnp.where(
        jnp.arange(slab_most * BLK, dtype=jnp.int32) < own_length * BLK, unit_norm, 0.0
    )
    summed = lax.psum_scatter(
        jnp.dot(attn_local, out_weight, preferred_element_type=jnp.float32).astype(jnp.bfloat16),
        ("sub", "rep"),
        scatter_dimension=0,
        tiled=True,
    )
    return (summed, unit_norm.reshape(1, 1, slab_most * BLK))


def solution(mesh):
    placed = (
        P(("grp", "seq"), ("sub", "rep")),
        P(("grp", "seq"), ("sub", "rep")),
        P(("grp", "seq"), ("sub", "rep")),
        P(("grp", "sub", "rep"), None, None),
        P(("grp", "sub", "rep"), None, None),
        P(("sub", "rep"), None),
    )
    return jax.shard_map(
        local,
        mesh=mesh,
        in_specs=placed,
        out_specs=(P(("grp", "seq", "sub", "rep"), None), P(("grp", "sub", "rep"), "seq", None)),
        check_vma=False,
    )
```

```python
import math

import jax
import jax.numpy as jnp
from jax import lax
from jax.sharding import PartitionSpec as P

DH = 128
BLK = 128


def around(piece, count):
    pieces = [piece]
    for shift in range(1, count):
        pairs = [(source, (source + shift) % count) for source in range(count)]
        pieces.append(lax.ppermute(piece, "seq", pairs))
    return pieces


def local(query_proj, key_proj, value_proj, block_mask, unit_plan, out_weight):
    tok_count = query_proj.shape[0]
    head_count = block_mask.shape[0]
    block_count = block_mask.shape[2]
    seq_index = lax.axis_index("seq")
    local_blocks = tok_count // BLK
    slab_most = min(2 * head_count * local_blocks, block_count)
    score_scale = 1.0 / math.sqrt(DH)
    seq_count = lax.axis_size("seq")
    key_value = jnp.stack([key_proj, value_proj], axis=0)
    gathered = jnp.concatenate(around(key_value, seq_count), axis=1)
    all_tokens = gathered.shape[1]
    sources = (seq_index - jnp.arange(seq_count, dtype=jnp.int32)) % seq_count
    column_order = (sources[:, None] * local_blocks + jnp.arange(local_blocks)[None, :]).reshape(-1)
    keys = gathered[0].reshape(all_tokens, head_count, DH)
    values = gathered[1].reshape(all_tokens, head_count, DH)
    queries = query_proj.reshape(tok_count, head_count, DH)
    scores = (
        jnp.einsum("thc,shc->hts", queries, keys, preferred_element_type=jnp.float32)
        * score_scale
    )
    own_rows = lax.dynamic_slice_in_dim(block_mask, seq_index * local_blocks, local_blocks, 1)
    own_rows = jnp.take(own_rows, column_order, axis=2)
    live = jnp.repeat(jnp.repeat(own_rows > 0, BLK, axis=1), BLK, axis=2)
    masked = jnp.where(live, scores, -jnp.inf)
    row_peak = jnp.max(masked, axis=2, keepdims=True)
    weights = jnp.where(live, jnp.exp(masked - row_peak), 0.0)
    row_total = jnp.sum(weights, axis=2, keepdims=True)
    mixed = (
        jnp.einsum(
            "hts,shc->htc",
            weights.astype(jnp.bfloat16),
            values,
            preferred_element_type=jnp.float32,
        )
        / row_total
    )
    attn_local = mixed.astype(jnp.bfloat16).transpose(1, 0, 2).reshape(tok_count, head_count * DH)
    lognorm = (row_peak + jnp.log(row_total))[:, :, 0]
    arrived = jnp.stack(around(lognorm, seq_count), axis=0)
    all_norm = jnp.take(arrived, (seq_index - jnp.arange(seq_count)) % seq_count, axis=0)
    all_norm = all_norm.transpose(1, 0, 2).reshape(head_count, seq_count * tok_count)
    own_head = unit_plan[0, seq_index, 0]
    own_first = unit_plan[0, seq_index, 1]
    own_length = unit_plan[0, seq_index, 2]
    head_norm = jnp.concatenate(
        [all_norm[own_head], jnp.zeros((slab_most * BLK,), jnp.float32)], axis=0
    )
    unit_norm = lax.dynamic_slice_in_dim(head_norm, own_first * BLK, slab_most * BLK, 0)
    unit_norm = jnp.where(
        jnp.arange(slab_most * BLK, dtype=jnp.int32) < own_length * BLK, unit_norm, 0.0
    )
    summed = lax.psum_scatter(
        jnp.dot(attn_local, out_weight, preferred_element_type=jnp.float32).astype(jnp.bfloat16),
        ("sub", "rep"),
        scatter_dimension=0,
        tiled=True,
    )
    return (summed, unit_norm.reshape(1, 1, slab_most * BLK))


def solution(mesh):
    placed = (
        P(("grp", "seq"), ("sub", "rep")),
        P(("grp", "seq"), ("sub", "rep")),
        P(("grp", "seq"), ("sub", "rep")),
        P(("grp", "sub", "rep"), None, None),
        P(("grp", "sub", "rep"), None, None),
        P(("sub", "rep"), None),
    )
    return jax.shard_map(
        local,
        mesh=mesh,
        in_specs=placed,
        out_specs=(P(("grp", "seq", "sub", "rep"), None), P(("grp", "sub", "rep"), "seq", None)),
        check_vma=False,
    )
```

```python
import math

import jax
import jax.numpy as jnp
from jax import lax
from jax.sharding import PartitionSpec as P

DH = 128
BLK = 128


def around(piece, count):
    pieces = [piece]
    for shift in range(1, count):
        pairs = [(source, (source + shift) % count) for source in range(count)]
        pieces.append(lax.ppermute(piece, "seq", pairs))
    return pieces


def local(query_proj, key_proj, value_proj, block_mask, unit_plan, out_weight):
    tok_count = query_proj.shape[0]
    head_count = block_mask.shape[0]
    block_count = block_mask.shape[2]
    seq_index = lax.axis_index("seq")
    local_blocks = tok_count // BLK
    slab_most = min(2 * head_count * local_blocks, block_count)
    score_scale = 1.0 / math.sqrt(DH)
    seq_count = lax.axis_size("seq")
    key_value = jnp.stack([key_proj, value_proj], axis=0)
    gathered = jnp.concatenate(around(key_value, seq_count), axis=1)
    all_tokens = gathered.shape[1]
    sources = (seq_index - jnp.arange(seq_count, dtype=jnp.int32)) % seq_count
    column_order = (sources[:, None] * local_blocks + jnp.arange(local_blocks)[None, :]).reshape(-1)
    keys = gathered[0].reshape(all_tokens, head_count, DH)
    values = gathered[1].reshape(all_tokens, head_count, DH)
    queries = query_proj.reshape(tok_count, head_count, DH)
    scores = (
        jnp.einsum("thc,shc->hts", queries, keys, preferred_element_type=jnp.float32)
        * score_scale
    )
    own_rows = lax.dynamic_slice_in_dim(block_mask, seq_index * local_blocks, local_blocks, 1)
    own_rows = jnp.take(own_rows, column_order, axis=2)
    live = jnp.repeat(jnp.repeat(own_rows > 0, BLK, axis=1), BLK, axis=2)
    masked = jnp.where(live, scores, -jnp.inf)
    row_peak = jnp.max(masked, axis=2, keepdims=True)
    weights = jnp.where(live, jnp.exp(masked - row_peak), 0.0)
    row_total = jnp.sum(weights, axis=2, keepdims=True)
    mixed = (
        jnp.einsum(
            "hts,shc->htc",
            weights.astype(jnp.bfloat16),
            values,
            preferred_element_type=jnp.float32,
        )
        / row_total
    )
    attn_local = mixed.astype(jnp.bfloat16).transpose(1, 0, 2).reshape(tok_count, head_count * DH)
    lognorm = (row_peak + jnp.log(row_total))[:, :, 0]
    arrived = jnp.stack(around(lognorm, seq_count), axis=0)
    all_norm = jnp.take(arrived, (seq_index - jnp.arange(seq_count)) % seq_count, axis=0)
    all_norm = all_norm.transpose(1, 0, 2).reshape(head_count, seq_count * tok_count)
    own_head = unit_plan[0, seq_index, 0]
    own_first = unit_plan[0, seq_index, 1]
    own_length = unit_plan[0, seq_index, 2]
    head_norm = jnp.concatenate(
        [all_norm[own_head], jnp.zeros((slab_most * BLK,), jnp.float32)], axis=0
    )
    unit_norm = lax.dynamic_slice_in_dim(head_norm, own_first * BLK, slab_most * BLK, 0)
    unit_norm = jnp.where(
        jnp.arange(slab_most * BLK, dtype=jnp.int32) < own_length * BLK, unit_norm, 0.0
    )
    partial = jnp.dot(attn_local, out_weight, preferred_element_type=jnp.float32)
    sub_count = lax.axis_size("sub")
    rep_count = lax.axis_size("rep")
    partial = partial.astype(jnp.bfloat16).reshape(
        sub_count, rep_count, tok_count // (sub_count * rep_count), partial.shape[1]
    )
    partial = lax.psum_scatter(partial.transpose(1, 0, 2, 3), "rep", scatter_dimension=0, tiled=True)
    summed = lax.psum_scatter(partial, "sub", scatter_dimension=1, tiled=True)
    summed = summed.reshape(summed.shape[0] * summed.shape[1] * summed.shape[2], summed.shape[3])
    return (summed, unit_norm.reshape(1, 1, slab_most * BLK))


def solution(mesh):
    placed = (
        P(("grp", "seq"), ("sub", "rep")),
        P(("grp", "seq"), ("sub", "rep")),
        P(("grp", "seq"), ("sub", "rep")),
        P(("grp", "sub", "rep"), None, None),
        P(("grp", "sub", "rep"), None, None),
        P(("sub", "rep"), None),
    )
    return jax.shard_map(
        local,
        mesh=mesh,
        in_specs=placed,
        out_specs=(P(("grp", "seq", "sub", "rep"), None), P(("grp", "sub", "rep"), "seq", None)),
        check_vma=False,
    )
```

```python
import math

import jax
import jax.numpy as jnp
from jax import lax
from jax.sharding import PartitionSpec as P

DH = 128
BLK = 128


def around(piece, count):
    pieces = [piece]
    for shift in range(1, count):
        pairs = [(source, (source + shift) % count) for source in range(count)]
        pieces.append(lax.ppermute(piece, "seq", pairs))
    return pieces


def local(query_proj, key_proj, value_proj, block_mask, unit_plan, out_weight):
    tok_count = query_proj.shape[0]
    head_count = block_mask.shape[0]
    block_count = block_mask.shape[2]
    seq_index = lax.axis_index("seq")
    local_blocks = tok_count // BLK
    slab_most = min(2 * head_count * local_blocks, block_count)
    score_scale = 1.0 / math.sqrt(DH)
    seq_count = lax.axis_size("seq")
    key_value = jnp.stack([key_proj, value_proj], axis=0)
    gathered = jnp.concatenate(around(key_value, seq_count), axis=1)
    all_tokens = gathered.shape[1]
    sources = (seq_index - jnp.arange(seq_count, dtype=jnp.int32)) % seq_count
    column_order = (sources[:, None] * local_blocks + jnp.arange(local_blocks)[None, :]).reshape(-1)
    keys = gathered[0].reshape(all_tokens, head_count, DH)
    values = gathered[1].reshape(all_tokens, head_count, DH)
    queries = query_proj.reshape(tok_count, head_count, DH)
    scores = (
        jnp.einsum("thc,shc->hts", queries, keys, preferred_element_type=jnp.float32)
        * score_scale
    )
    own_rows = lax.dynamic_slice_in_dim(block_mask, seq_index * local_blocks, local_blocks, 1)
    own_rows = jnp.take(own_rows, column_order, axis=2)
    live = jnp.repeat(jnp.repeat(own_rows > 0, BLK, axis=1), BLK, axis=2)
    masked = jnp.where(live, scores, -jnp.inf)
    row_peak = jnp.max(masked, axis=2, keepdims=True)
    weights = jnp.where(live, jnp.exp(masked - row_peak), 0.0)
    row_total = jnp.sum(weights, axis=2, keepdims=True)
    mixed = (
        jnp.einsum(
            "hts,shc->htc",
            weights.astype(jnp.bfloat16),
            values,
            preferred_element_type=jnp.float32,
        )
        / row_total
    )
    attn_local = mixed.astype(jnp.bfloat16).transpose(1, 0, 2).reshape(tok_count, head_count * DH)
    lognorm = (row_peak + jnp.log(row_total))[:, :, 0]
    arrived = jnp.stack(around(lognorm, seq_count), axis=0)
    all_norm = jnp.take(arrived, (seq_index - jnp.arange(seq_count)) % seq_count, axis=0)
    all_norm = all_norm.transpose(1, 0, 2).reshape(head_count, seq_count * tok_count)
    own_head = unit_plan[0, seq_index, 0]
    own_first = unit_plan[0, seq_index, 1]
    own_length = unit_plan[0, seq_index, 2]
    head_norm = jnp.concatenate(
        [all_norm[own_head], jnp.zeros((slab_most * BLK,), jnp.float32)], axis=0
    )
    unit_norm = lax.dynamic_slice_in_dim(head_norm, own_first * BLK, slab_most * BLK, 0)
    unit_norm = jnp.where(
        jnp.arange(slab_most * BLK, dtype=jnp.int32) < own_length * BLK, unit_norm, 0.0
    )
    partial = jnp.dot(attn_local, out_weight, preferred_element_type=jnp.float32)
    rep_count = lax.axis_size("rep")
    peer_count = lax.axis_size("sub") * rep_count
    peer_index = lax.axis_index("sub") * rep_count + lax.axis_index("rep")
    chunk = tok_count // peer_count
    chunks = partial.astype(jnp.bfloat16).reshape(peer_count, chunk, partial.shape[1])
    summed = partial.reshape(peer_count, chunk, partial.shape[1])[peer_index]
    for shift in range(1, peer_count):
        pairs = [(source, (source + shift) % peer_count) for source in range(peer_count)]
        sent = chunks[(peer_index + shift) % peer_count]
        summed = summed + lax.ppermute(sent, ("sub", "rep"), pairs).astype(jnp.float32)
    return (summed.astype(jnp.bfloat16), unit_norm.reshape(1, 1, slab_most * BLK))


def solution(mesh):
    placed = (
        P(("grp", "seq"), ("sub", "rep")),
        P(("grp", "seq"), ("sub", "rep")),
        P(("grp", "seq"), ("sub", "rep")),
        P(("grp", "sub", "rep"), None, None),
        P(("grp", "sub", "rep"), None, None),
        P(("sub", "rep"), None),
    )
    return jax.shard_map(
        local,
        mesh=mesh,
        in_specs=placed,
        out_specs=(P(("grp", "seq", "sub", "rep"), None), P(("grp", "sub", "rep"), "seq", None)),
        check_vma=False,
    )
```

```python
import math

import jax
import jax.numpy as jnp
from jax import lax
from jax.sharding import PartitionSpec as P

DH = 128
BLK = 128


def around(piece, count):
    pieces = [piece]
    for shift in range(1, count):
        pairs = [(source, (source + shift) % count) for source in range(count)]
        pieces.append(lax.ppermute(piece, "seq", pairs))
    return pieces


def local(query_proj, key_proj, value_proj, block_mask, unit_plan, out_weight):
    tok_count = query_proj.shape[0]
    head_count = block_mask.shape[0]
    block_count = block_mask.shape[2]
    seq_index = lax.axis_index("seq")
    local_blocks = tok_count // BLK
    slab_most = min(2 * head_count * local_blocks, block_count)
    score_scale = 1.0 / math.sqrt(DH)
    seq_count = lax.axis_size("seq")
    key_value = jnp.stack([key_proj, value_proj], axis=0)
    gathered = jnp.concatenate(around(key_value, seq_count), axis=1)
    all_tokens = gathered.shape[1]
    sources = (seq_index - jnp.arange(seq_count, dtype=jnp.int32)) % seq_count
    column_order = (sources[:, None] * local_blocks + jnp.arange(local_blocks)[None, :]).reshape(-1)
    keys = gathered[0].reshape(all_tokens, head_count, DH)
    values = gathered[1].reshape(all_tokens, head_count, DH)
    queries = query_proj.reshape(tok_count, head_count, DH)
    scores = (
        jnp.einsum("thc,shc->hts", queries, keys, preferred_element_type=jnp.float32)
        * score_scale
    )
    own_rows = lax.dynamic_slice_in_dim(block_mask, seq_index * local_blocks, local_blocks, 1)
    own_rows = jnp.take(own_rows, column_order, axis=2)
    live = jnp.repeat(jnp.repeat(own_rows > 0, BLK, axis=1), BLK, axis=2)
    masked = jnp.where(live, scores, -jnp.inf)
    row_peak = jnp.max(masked, axis=2, keepdims=True)
    weights = jnp.where(live, jnp.exp(masked - row_peak), 0.0)
    row_total = jnp.sum(weights, axis=2, keepdims=True)
    mixed = (
        jnp.einsum(
            "hts,shc->htc",
            weights.astype(jnp.bfloat16),
            values,
            preferred_element_type=jnp.float32,
        )
        / row_total
    )
    attn_local = mixed.astype(jnp.bfloat16).transpose(1, 0, 2).reshape(tok_count, head_count * DH)
    lognorm = (row_peak + jnp.log(row_total))[:, :, 0]
    arrived = jnp.stack(around(lognorm, seq_count), axis=0)
    all_norm = jnp.take(arrived, (seq_index - jnp.arange(seq_count)) % seq_count, axis=0)
    all_norm = all_norm.transpose(1, 0, 2).reshape(head_count, seq_count * tok_count)
    own_head = unit_plan[0, seq_index, 0]
    own_first = unit_plan[0, seq_index, 1]
    own_length = unit_plan[0, seq_index, 2]
    head_norm = jnp.concatenate(
        [all_norm[own_head], jnp.zeros((slab_most * BLK,), jnp.float32)], axis=0
    )
    unit_norm = lax.dynamic_slice_in_dim(head_norm, own_first * BLK, slab_most * BLK, 0)
    unit_norm = jnp.where(
        jnp.arange(slab_most * BLK, dtype=jnp.int32) < own_length * BLK, unit_norm, 0.0
    )
    rep_count = lax.axis_size("rep")
    peer_count = lax.axis_size("sub") * rep_count
    peer_index = lax.axis_index("sub") * rep_count + lax.axis_index("rep")
    chunk = tok_count // peer_count
    received = []
    for shift in range(1, peer_count):
        pairs = [(source, (source + shift) % peer_count) for source in range(peer_count)]
        rows = lax.dynamic_slice_in_dim(
            attn_local, ((peer_index + shift) % peer_count) * chunk, chunk, 0
        )
        sent = jnp.dot(rows, out_weight, preferred_element_type=jnp.float32)
        received.append(lax.ppermute(sent.astype(jnp.bfloat16), ("sub", "rep"), pairs))
    own_rows = lax.dynamic_slice_in_dim(attn_local, peer_index * chunk, chunk, 0)
    summed = jnp.dot(own_rows, out_weight, preferred_element_type=jnp.float32)
    for piece in received:
        summed = summed + piece.astype(jnp.float32)
    return (summed.astype(jnp.bfloat16), unit_norm.reshape(1, 1, slab_most * BLK))


def solution(mesh):
    placed = (
        P(("grp", "seq"), ("sub", "rep")),
        P(("grp", "seq"), ("sub", "rep")),
        P(("grp", "seq"), ("sub", "rep")),
        P(("grp", "sub", "rep"), None, None),
        P(("grp", "sub", "rep"), None, None),
        P(("sub", "rep"), None),
    )
    return jax.shard_map(
        local,
        mesh=mesh,
        in_specs=placed,
        out_specs=(P(("grp", "seq", "sub", "rep"), None), P(("grp", "sub", "rep"), "seq", None)),
        check_vma=False,
    )
```
